32 devices in a mesh: grp: 2 (over y), ctx: 4 (over z), sub: 4 (over x, core).
Axes of the slice: x: 2, y: 2, z: 4, core: 2. Of those that a mesh axis runs over, the one named last changes fastest.
Arguments:
- queries: bfloat16 [64, 3072], P(('grp', 'ctx'), 'sub'), parts along dimension 0, may hold values from -1024 to 1024
- latent_cache: bfloat16 [3072, 576], P(('grp', 'ctx')), parts along dimension 0, may hold values from -8 to 8
- cache_len: int32 [8], P(('grp', 'ctx')), parts along dimension 0, may hold values from 16 to 384, as said below
- kv_up: bfloat16 [32, 256, 512], P(('grp', 'sub'), None, 'ctx'), parts along dimension 0, may hold values from -1 to 1
- o_weight: bfloat16 [2048, 2048], P('sub', 'ctx'), may hold values from -0.5 to 0.5
- residual: bfloat16 [64, 2048], P(('grp', 'ctx')), parts along dimension 0, may hold values from -3 to 3
- norm_gain: bfloat16 [2048], replicated, may hold values from 0.25 to 1.75
- route_ids: int32 [64, 6], P(('grp', 'ctx')), parts along dimension 0, may hold values from 0 to 63, all different within a row; in each aligned block of 8 rows (0 to 7, 8 to 15, ...) at most 2 rows name the same one
- route_weights: float32 [64, 6], P(('grp', 'ctx')), parts along dimension 0, may hold values from 0.1 to 0.6
- w_gate: bfloat16 [64, 2048, 1408], P('ctx', None, 'sub'), may hold values from -0.125 to 0.125
- w_up: bfloat16 [64, 2048, 1408], P('ctx', None, 'sub'), may hold values from -0.125 to 0.125
- w_down: bfloat16 [64, 1408, 2048], P('ctx', 'sub'), may hold values from -0.15625 to 0.15625
Outputs:
- layer_out: bfloat16 [64, 2048], P(('grp', 'ctx'), 'sub'), parts along dimension 0
The draws below stay inside these ranges and needn't reach their ends.
There are 2 independent parts, one for each index of `grp`. The reference program is written for one: setup_inputs(seed, part) draws one part's arguments, and reference() takes and returns one part's arrays. A program takes and returns all parts, laid end to end along the dimension named above; an argument that names none is the same for every part. Nothing has to cross between parts.
Inputs may be any that keep to these rules, and one draw needn't show every extreme that they name: `route_ids`: each row names 6 different experts. Among the 8 rows of one ctx index no expert is named more than 2 times, and in every draw some expert is named exactly 2 times by the rows of some ctx index. cache_len[c] positions at the start of shard c are live; at least one shard is full.
All inputs are finite; a program needn't handle non-finite values.
Results may differ from the reference program's by a relative error of at most 0.015.
Values may be sent and summed in bfloat16 or wider, within the bound.
A program may use at most 128 MiB of HBM per device.

```python
import math
import jax
import jax.numpy as jnp
import numpy as np
from jax import lax

D = 2048
HEADS = 16
NOPE = 128
ROPE = 64
VDIM = 128
LATENT = 512
FF = 1408
EXPERTS = 64
TOP = 6
TOK_DEV = 8
CACHE_DEV = 384
CAP = 2
SPAN = 32
CACHE = 1536
N_CTX = 4


def draw_tables(key):
    base_key = jax.random.fold_in(key, 7)
    cache_key, up_key, query_key = jax.random.split(base_key, 3)
    row_width = LATENT + ROPE
    cache_rows = jnp.clip(jax.random.normal(cache_key, (CACHE, row_width), jnp.float32), -6.0, 6.0)
    up_table = jnp.clip(jax.random.normal(up_key, (HEADS, NOPE + VDIM, LATENT), jnp.float32), -6.0, 6.0) * LATENT ** (-0.5)
    query_table = jnp.clip(jax.random.normal(query_key, (SPAN, HEADS, NOPE + ROPE), jnp.float32), -6.0, 6.0) * 2.5
    return (cache_rows, up_table, query_table)


def draw_queries(key, part):
    tables = draw_tables(key)
    return tables[2].reshape(SPAN, HEADS * (NOPE + ROPE)).astype(jnp.bfloat16)


def draw_latent_cache(key, part):
    tables = draw_tables(key)
    return tables[0].astype(jnp.bfloat16)


def draw_kv_up(key, part):
    tables = draw_tables(key)
    return tables[1].astype(jnp.bfloat16)


def draw_cache_len(key, part):
    length_key, full_key = jax.random.split(jax.random.fold_in(key, 11))
    halvings = jax.random.randint(length_key, (N_CTX,), 0, 5)
    lengths = jnp.maximum(jnp.right_shift(jnp.full((N_CTX,), CACHE_DEV, jnp.int32), halvings.astype(jnp.int32)), 16)
    full_index = jax.random.randint(full_key, (), 0, N_CTX)
    return jnp.where(jnp.arange(N_CTX, dtype=jnp.int32) == full_index, CACHE_DEV, lengths).astype(jnp.int32)


def shard_levels(key, dims, cuts, least, top_value):
    def one(position, blocks):
        draws = jax.random.uniform(jax.random.fold_in(jax.random.fold_in(key, 6), position), (blocks,), jnp.float32, least / len(cuts), top_value / len(cuts))
        return jnp.repeat(jnp.exp(draws), dims[position] // blocks).reshape((-1,) + (1,) * (len(dims) - position - 1))

    gain = one(*cuts[0])
    for cut in cuts[1:]:
        gain = gain * one(*cut)
    return gain


def assign_block(rng, own, number, rows, count, top, bound, lean):
    ranking = jax.random.permutation(rng, count)
    packed, usual = portions_of(count, rows * top, bound, lean, True), portions_of(count, rows * top, bound, lean, False)
    places = jnp.arange(count)

    def named(sizes, rotation):
        used = int((sizes > 0).sum())
        fixed = max(1, used // 4)
        moved = fixed + (places - fixed + rotation * (used - fixed)) % max(1, count - fixed)
        return jnp.zeros((count,), jnp.int32).at[ranking[jnp.where(places < fixed, places, moved)]].set(jnp.asarray(sizes, jnp.int32))

    sizes = jnp.where(number % 4 == 0, named(packed, number // 4), named(usual, number - number // 4 - 1))
    mixed = jax.random.permutation(jax.random.fold_in(own, 3), count)
    giver, sink = mixed[0:count // 2 * 2:2], mixed[1:count // 2 * 2:2]
    margin = jnp.minimum(sizes[giver] - 1, bound - sizes[sink]) // 2
    margin = jnp.where((giver == ranking[0]) | (sink == ranking[0]) | (sizes[sink] == 0), 0, jnp.maximum(margin, 0))
    moved = jax.random.randint(jax.random.fold_in(own, 4), (count // 2,), 0, 1 << 20) % (margin + 1)
    sizes = sizes.at[giver].add(-moved).at[sink].add(moved)
    items = jnp.searchsorted(jnp.cumsum(sizes), jnp.arange(rows * top), side="right").astype(jnp.int32)
    table = items.reshape(top, rows).T
    table = table[jax.random.permutation(jax.random.fold_in(own, 1), rows)]
    rotation = jax.random.randint(jax.random.fold_in(own, 2), (rows, 1), 0, top)
    return jnp.take_along_axis(table, (jnp.arange(top)[None, :] + rotation) % top, axis=1)


def portions_of(number_of, total, bound, lean, full):
    loads = [(1 << 20) // math.isqrt(standing ** lean) + 1 for standing in range(1, number_of + 1)]
    largest = bound if full else min(bound, max(-(-total // number_of), total * loads[0] // sum(loads)))
    least = 1 if total - largest >= number_of - 1 else 0
    counts, spare = [largest] + [least] * (number_of - 1), total - largest - least * (number_of - 1)
    while spare > 0:
        movable = [i for i in range(1, number_of) if counts[i] < largest] or [i for i in range(1, number_of) if counts[i] < bound]
        pool, budget = sum([loads[i] for i in movable]), spare
        for i in movable:
            extra = min(bound - counts[i], max(1, budget * loads[i] // pool), spare)
            counts[i] = counts[i] + extra
            spare = spare - extra
    return np.array(counts)


def bell_draw(key, extent, spread, reach, cuts=(), kind=jnp.bfloat16):
    loudness = shard_levels(key, extent, cuts, -0.22, 0.18) if cuts else 1.0
    array = jax.random.normal(key, extent, jnp.float32) * spread * loudness
    return jnp.minimum(jnp.maximum(array, -reach), reach).astype(kind)


def setup_inputs(seed: int = 0, part: int = 0) -> dict:
    keys = jax.random.split(jax.random.key(seed), 13)
    part_keys = jax.random.split(jax.random.fold_in(keys[12], part), 13)
    queries = draw_queries(jax.random.fold_in(jax.random.fold_in(keys[12], part), 71), part)
    latent_cache = draw_latent_cache(jax.random.fold_in(jax.random.fold_in(keys[12], part), 71), part)
    cache_len = draw_cache_len(jax.random.fold_in(jax.random.fold_in(keys[12], part), 71), part)
    kv_up = draw_kv_up(jax.random.fold_in(jax.random.fold_in(keys[12], part), 71), part)
    o_weight = bell_draw(keys[4], (HEADS * VDIM, D), (HEADS * VDIM // 16) ** -0.5, 0.5, ((0, 4), (1, 4)))
    residual = bell_draw(part_keys[5], (SPAN, D), 0.5, 3.0, ((0, 4),))
    norm_gain = jnp.clip(1.0 + 0.15 * jax.random.normal(keys[6], (D,), jnp.float32), 0.25, 1.75).astype(jnp.bfloat16)
    route_ids_keys = jax.random.split(jax.random.fold_in(part_keys[7], 1), SPAN // TOK_DEV)
    route_ids_turns = jax.random.permutation(jax.random.fold_in(part_keys[7], 3), SPAN // TOK_DEV)
    route_ids = jax.vmap(lambda own, number: assign_block(jax.random.fold_in(part_keys[7], 2), own, number, TOK_DEV, EXPERTS, TOP, CAP, 2))(route_ids_keys, route_ids_turns).reshape((SPAN, TOP))
    route_weights = jnp.clip(0.1 + 0.5 * jax.random.uniform(part_keys[8], (SPAN, TOP), jnp.float32) ** shard_levels(part_keys[8], (SPAN, TOP), ((0, 4),), -0.2, 0.2), 0.1, 0.6)
    w_gate = bell_draw(keys[9], (EXPERTS, D, FF), D ** -0.5, 0.125, ((0, 4), (2, 4)))
    w_up = bell_draw(keys[10], (EXPERTS, D, FF), D ** -0.5, 0.125, ((0, 4), (2, 4)))
    w_down = bell_draw(keys[11], (EXPERTS, FF, D), FF ** -0.5, 0.15625, ((0, 4), (1, 4)))
    return dict(queries=queries, latent_cache=latent_cache, cache_len=cache_len, kv_up=kv_up, o_weight=o_weight, residual=residual, norm_gain=norm_gain, route_ids=route_ids, route_weights=route_weights, w_gate=w_gate, w_up=w_up, w_down=w_down)


epsilon = 1e-06

def shard_attention(absorbed, cache_rows, live_mask, up_value):
    scores = jnp.einsum('qhc,kc->qhk', absorbed.astype(jnp.float32), cache_rows.astype(jnp.float32)) * (NOPE + ROPE) ** (-0.5)
    scores = jnp.where(live_mask[None, None, :], scores, -jnp.inf)
    highest = lax.optimization_barrier(jnp.max(scores, axis=2))
    weights = jnp.exp(scores - highest[:, :, None]).astype(jnp.bfloat16)
    totals = lax.optimization_barrier(jnp.sum(weights.astype(jnp.float32), axis=2))
    latent_out = jnp.einsum('qhk,kl->qhl', weights.astype(jnp.float32), cache_rows[:, :LATENT].astype(jnp.float32)).astype(jnp.bfloat16)
    head_out = jnp.einsum('qhl,hvl->qhv', latent_out.astype(jnp.float32), up_value.astype(jnp.float32))
    return (highest, totals, head_out)

def reference(queries, latent_cache, cache_len, kv_up, o_weight, residual, norm_gain, route_ids, route_weights, w_gate, w_up, w_down):
    query_heads = queries.reshape(SPAN, HEADS, NOPE + ROPE)
    query_latent = jnp.einsum('qhn,hnl->qhl', query_heads[:, :, :NOPE].astype(jnp.float32), kv_up[:, :NOPE, :].astype(jnp.float32)).astype(jnp.bfloat16)
    absorbed = jnp.concatenate([query_latent, query_heads[:, :, NOPE:]], axis=2)
    up_value = kv_up[:, NOPE:, :]
    blocks = latent_cache.reshape(N_CTX, CACHE_DEV, LATENT + ROPE)
    positions = jnp.arange(CACHE_DEV, dtype=jnp.int32)

    def fold_shard(running, shard_item):
        highest, totals, summed = running
        cache_rows, length = shard_item
        shard_high, shard_total, shard_head = shard_attention(absorbed, cache_rows, positions < length, up_value)
        new_high = jnp.maximum(highest, shard_high)
        old_factor = jnp.exp(highest - new_high)
        new_factor = jnp.exp(shard_high - new_high)
        return ((new_high, totals * old_factor + shard_total * new_factor, summed * old_factor[:, :, None] + shard_head * new_factor[:, :, None]), None)
    initial = (jnp.full((SPAN, HEADS), -jnp.inf, jnp.float32), jnp.zeros((SPAN, HEADS), jnp.float32), jnp.zeros((SPAN, HEADS, VDIM), jnp.float32))
    (highest, totals, summed), unused = lax.scan(fold_shard, initial, (blocks, cache_len))
    attention = (summed / totals[:, :, None]).astype(jnp.bfloat16).reshape(SPAN, HEADS * VDIM)
    hidden = residual.astype(jnp.float32) + jnp.dot(attention, o_weight, preferred_element_type=jnp.float32)
    inverse_rms = lax.rsqrt(lax.optimization_barrier(jnp.mean(hidden * hidden, axis=1)) + epsilon)
    normed = (hidden * inverse_rms[:, None] * norm_gain.astype(jnp.float32)).astype(jnp.bfloat16)
    pair_count = TOK_DEV * TOP
    expert_ids = route_ids.reshape(N_CTX, pair_count)
    onehot = (expert_ids[:, :, None] == jnp.arange(EXPERTS, dtype=jnp.int32)[None, None, :]).astype(jnp.int32)
    earlier = jnp.cumsum(onehot, axis=1) - onehot
    slot_ids = lax.optimization_barrier(jnp.sum(earlier * onehot, axis=2))
    targets = (expert_ids * CAP + slot_ids).reshape(N_CTX, TOK_DEV, TOP)
    columns = jnp.arange(EXPERTS * CAP, dtype=jnp.int32)
    matches = targets[:, :, :, None] == columns[None, None, None, :]
    select = lax.optimization_barrier(jnp.sum(matches.astype(jnp.float32), axis=2))
    normed_blocks = normed.reshape(N_CTX, TOK_DEV, D)
    dispatched = jnp.einsum('ctj,ctd->cjd', select, normed_blocks.astype(jnp.float32)).astype(jnp.bfloat16)
    by_expert = dispatched.reshape(N_CTX, EXPERTS, CAP, D).transpose(1, 0, 2, 3).reshape(EXPERTS, N_CTX * CAP, D)

    def run_expert(operands):
        rows_in, gate_matrix, up_matrix, down_matrix = operands
        gate_act = jnp.dot(rows_in, gate_matrix, preferred_element_type=jnp.float32)
        up_act = jnp.dot(rows_in, up_matrix, preferred_element_type=jnp.float32)
        gated_rows = (jax.nn.silu(gate_act) * up_act).astype(jnp.bfloat16)
        return jnp.dot(gated_rows, down_matrix, preferred_element_type=jnp.float32).astype(jnp.bfloat16)
    expert_out = lax.map(run_expert, (by_expert, w_gate, w_up, w_down))
    back_rows = expert_out.reshape(EXPERTS, N_CTX, CAP, D).transpose(1, 0, 2, 3).reshape(N_CTX, EXPERTS * CAP, D)
    mixing = lax.optimization_barrier(jnp.sum(jnp.where(matches, route_weights.reshape(N_CTX, TOK_DEV, TOP)[:, :, :, None], 0.0), axis=2))
    routed = jnp.einsum('ctj,cjd->ctd', mixing, back_rows.astype(jnp.float32), precision=lax.Precision.HIGHEST)
    return (hidden + routed.reshape(SPAN, D)).astype(jnp.bfloat16)
```

```python
import functools

import jax
import jax.numpy as jnp
from jax import lax
from jax.experimental import pallas as pl
from jax.experimental.pallas import tpu as pltpu
from jax.sharding import PartitionSpec as P

D = 2048
NOPE = 128
ROPE = 64
VDIM = 128
LATENT = 512
TOP = 6
CAP = 2


epsilon = 1e-06


def local_attention(absorbed, cache_rows, length, up_value):
    scores = jnp.einsum("qhc,kc->qhk", absorbed, cache_rows, preferred_element_type=jnp.float32) * (
        NOPE + ROPE
    ) ** (-0.5)
    live_mask = lax.broadcasted_iota(jnp.int32, (cache_rows.shape[0],), 0) < length
    scores = jnp.where(live_mask[None, None, :], scores, -jnp.inf)
    highest = jnp.max(scores, axis=2)
    weights = jnp.exp(scores - highest[:, :, None]).astype(jnp.bfloat16)
    totals = jnp.sum(weights, axis=2, dtype=jnp.float32)
    latent_out = jnp.einsum(
        "qhk,kl->qhl", weights, cache_rows[:, :LATENT], preferred_element_type=jnp.float32
    ).astype(jnp.bfloat16)
    head_out = jnp.einsum("qhl,hvl->qhv", latent_out, up_value, preferred_element_type=jnp.float32)
    return (highest, totals, head_out)


def body(
    queries,
    latent_cache,
    cache_len,
    kv_up,
    o_weight,
    residual,
    norm_gain,
    route_ids,
    route_weights,
    w_gate,
    w_up,
    w_down,
):
    ctx_count = lax.axis_size("ctx")
    sub_count = lax.axis_size("sub")
    heads_dev = kv_up.shape[0]
    token_count = queries.shape[0]
    up_full = lax.all_gather(kv_up, "ctx", axis=2, tiled=True)
    up_key = up_full[:, :NOPE, :]
    up_value = up_full[:, NOPE:, :]
    own_rows = queries.reshape(token_count, heads_dev, NOPE + ROPE)
    query_latent = jnp.einsum(
        "qhn,hnl->qhl", own_rows[:, :, :NOPE], up_key, preferred_element_type=jnp.float32
    ).astype(jnp.bfloat16)
    mine = jnp.concatenate([query_latent, own_rows[:, :, NOPE:]], axis=2).reshape(
        token_count, heads_dev * (LATENT + ROPE)
    )
    absorbed = lax.all_gather(mine, "ctx", axis=0, tiled=True).reshape(-1, heads_dev, LATENT + ROPE)
    highest, totals, head_out = local_attention(absorbed, latent_cache, cache_len[0], up_value)
    all_rows = absorbed.shape[0]
    got_out, got_high, got_total = (
        lax.all_to_all(
            head_out.reshape(all_rows, heads_dev * VDIM),
            "ctx",
            split_axis=0,
            concat_axis=0,
            tiled=True,
        ),
        lax.all_to_all(highest, "ctx", split_axis=0, concat_axis=0, tiled=True),
        lax.all_to_all(totals, "ctx", split_axis=0, concat_axis=0, tiled=True),
    )
    got_out = got_out.reshape(ctx_count, token_count, heads_dev, VDIM)
    got_high = got_high.reshape(ctx_count, token_count, heads_dev)
    got_total = got_total.reshape(ctx_count, token_count, heads_dev)
    overall = jnp.max(got_high, axis=0)
    factor = jnp.exp(got_high - overall[None])
    numerator = jnp.sum(got_out * factor[:, :, :, None], axis=0)
    denominator = jnp.sum(got_total * factor, axis=0)
    attention = (
        (numerator / denominator[:, :, None])
        .astype(jnp.bfloat16)
        .reshape(token_count, heads_dev * VDIM)
    )
    projected = jnp.dot(
        attention,
        lax.all_gather(o_weight, "ctx", axis=1, tiled=True),
        preferred_element_type=jnp.float32,
    )
    quarter = D // sub_count
    offset_cols = lax.axis_index("sub") * quarter
    hidden = residual.astype(jnp.float32) + lax.psum(projected.astype(jnp.bfloat16), "sub").astype(
        jnp.float32
    )
    inverse_rms = lax.rsqrt(jnp.mean(hidden * hidden, axis=1) + epsilon)
    normed = (hidden * inverse_rms[:, None] * norm_gain.astype(jnp.float32)).astype(jnp.bfloat16)
    hidden_part = lax.dynamic_slice_in_dim(hidden, offset_cols, quarter, 1)
    experts_dev = w_gate.shape[0]
    expert_total = experts_dev * ctx_count
    pair_count = token_count * TOP
    expert_ids = route_ids.reshape(pair_count)
    onehot = (expert_ids[:, None] == lax.broadcasted_iota(jnp.int32, (1, expert_total), 1)).astype(
        jnp.int32
    )
    earlier = jnp.cumsum(onehot, axis=0) - onehot
    slot_ids = jnp.sum(earlier * onehot, axis=1)
    targets = (expert_ids * CAP + slot_ids).reshape(token_count, TOP)
    matches = targets[:, :, None] == lax.broadcasted_iota(jnp.int32, (1, 1, expert_total * CAP), 2)
    select = jnp.sum(matches.astype(jnp.int32), axis=1).astype(jnp.bfloat16)
    outgoing = jnp.einsum("tj,td->jd", select, normed, preferred_element_type=jnp.float32).astype(
        jnp.bfloat16
    )
    outgoing = outgoing.reshape(ctx_count, experts_dev, CAP, D)
    received = lax.all_to_all(outgoing, "ctx", split_axis=0, concat_axis=0, tiled=True)
    gate_act = jnp.einsum("sekd,edf->sekf", received, w_gate, preferred_element_type=jnp.float32)
    up_act = jnp.einsum("sekd,edf->sekf", received, w_up, preferred_element_type=jnp.float32)
    gated_rows = (jax.nn.silu(gate_act) * up_act).astype(jnp.bfloat16)
    partial_out = jnp.einsum(
        "sekf,efd->sekd", gated_rows, w_down, preferred_element_type=jnp.float32
    )
    summed = lax.psum_scatter(
        partial_out.astype(jnp.bfloat16), "sub", scatter_dimension=3, tiled=True
    )
    back_rows = lax.all_to_all(summed, "ctx", split_axis=0, concat_axis=0, tiled=True)
    back_rows = back_rows.reshape(expert_total * CAP, quarter)
    mixing = jnp.sum(jnp.where(matches, route_weights[:, :, None], 0.0), axis=1)
    routed = jnp.dot(mixing, back_rows.astype(jnp.float32), precision=lax.Precision.HIGHEST)
    return (hidden_part + routed).astype(jnp.bfloat16)


LANES = 128
SLOTS = 12
MESH = pl.DeviceIdType.MESH
F32 = jnp.float32
BF16 = jnp.bfloat16


def fused_kernel(
    dims,
    pack_ref,
    live_ref,
    cache_ref,
    kv_ref,
    o_ref,
    gain_ref,
    gate_hbm,
    up_hbm,
    down_hbm,
    out_ref,
    pack_all,
    ql_send,
    ql_all,
    lat_send,
    lat_all,
    stat_send,
    stat_all,
    att_send,
    att_all,
    proj_send,
    proj_all,
    hid_send,
    hid_all,
    normed,
    total,
    fin_send,
    fin_all,
    gate_buf,
    up_buf,
    down_buf,
    ctx_send,
    ctx_recv,
    sub_send,
    sub_recv,
    fin_ssem,
    fin_rsem,
    w_sem,
):
    ctx, sub, tok, heads, experts, slots = dims
    me_c = lax.axis_index("ctx")
    me_s = lax.axis_index("sub")
    span = ctx * tok
    rows = heads * span
    quarter = o_ref.shape[1]

    def weight_copies(e, slot):
        return (
            pltpu.make_async_copy(gate_hbm.at[e], gate_buf.at[slot], w_sem.at[slot, 0]),
            pltpu.make_async_copy(up_hbm.at[e], up_buf.at[slot], w_sem.at[slot, 1]),
            pltpu.make_async_copy(down_hbm.at[e], down_buf.at[slot], w_sem.at[slot, 2]),
        )

    def prefetch(e, carry):
        for copy in weight_copies(e, e):
            copy.start()
        return carry

    lax.fori_loop(0, slots, prefetch, 0)

    barrier = pltpu.get_barrier_semaphore()
    for dc in range(ctx):
        for ds in range(sub):
            if dc or ds:
                pl.semaphore_signal(
                    barrier,
                    inc=1,
                    device_id={"ctx": lax.rem(me_c + dc, ctx), "sub": lax.rem(me_s + ds, sub)},
                    device_id_type=MESH,
                )
    pl.semaphore_wait(barrier, ctx * sub - 1)

    def ctx_copy(phase, source_of, target, d):
        peer = lax.rem(me_c + d, ctx)
        return pltpu.make_async_remote_copy(
            src_ref=source_of(peer),
            dst_ref=target.at[me_c],
            send_sem=ctx_send.at[phase, d],
            recv_sem=ctx_recv.at[phase, d],
            device_id={"ctx": peer},
            device_id_type=MESH,
        )

    def ctx_start(phase, source_of, target):
        copies = [ctx_copy(phase, source_of, target, d) for d in range(1, ctx)]
        for copy in copies:
            copy.start()
        return copies

    def finish(copies):
        for copy in copies:
            copy.wait()

    copies = ctx_start(0, lambda peer: pack_ref.at[peer], pack_all)
    pack_all[me_c] = pack_ref[me_c]
    finish(copies)

    for h in range(heads):
        nope = pack_all[:, :, h * 2 * LANES : h * 2 * LANES + NOPE].reshape(span, NOPE).astype(BF16)
        part = jnp.dot(nope, kv_ref[h, :NOPE, :], preferred_element_type=F32).astype(BF16)
        ql_send[h * span : (h + 1) * span, :] = part
    copies = ctx_start(1, lambda peer: ql_send, ql_all)
    ql_all[me_c] = ql_send[...]
    rope = jnp.concatenate(
        [
            pack_all[:, :, (2 * h + 1) * LANES : (2 * h + 1) * LANES + ROPE].reshape(span, ROPE)
            for h in range(heads)
        ],
        axis=0,
    ).astype(BF16)
    nt = (((1,), (1,)), ((), ()))
    rope_scores = lax.dot_general(rope, cache_ref[:, LATENT:], nt, preferred_element_type=F32)
    finish(copies)
    lat_q = jnp.concatenate([ql_all[c] for c in range(ctx)], axis=1)
    scores = lax.dot_general(lat_q, cache_ref[:, :LATENT], nt, preferred_element_type=F32)
    scores = (scores + rope_scores) * (NOPE + ROPE) ** (-0.5)
    scores = jnp.where(live_ref[...] > 0.0, scores, -jnp.inf)
    highest = jnp.max(scores, axis=1, keepdims=True)
    weights = jnp.exp(scores - highest).astype(BF16)
    totals = jnp.sum(weights.astype(F32), axis=1, keepdims=True)
    lane = lax.broadcasted_iota(jnp.int32, (rows, LANES), 1)
    stats = jnp.where(lane < 64, highest, totals).T
    stat_send[0:8, :] = stats[0:8, :]
    stat_send[8:16, :] = stats[64:72, :]
    copies = ctx_start(3, lambda peer: stat_send, stat_all)
    stat_all[me_c] = stat_send[...]
    latent = jnp.dot(weights, cache_ref[:, :LATENT], preferred_element_type=F32).astype(BF16)
    for c in range(ctx):
        lat_send[c] = latent[:, c * LANES : (c + 1) * LANES]
    copies += ctx_start(2, lambda peer: lat_send.at[peer], lat_all)
    lat_all[me_c] = lat_send[me_c]
    finish(copies)

    highs = [stat_all[c, 0:1, :] for c in range(ctx)]
    overall = functools.reduce(jnp.maximum, highs)
    factors = [jnp.exp(high - overall) for high in highs]
    denominator = sum(f * stat_all[c, 8:9, :] for c, f in enumerate(factors))
    merged = jnp.zeros((rows, LANES), F32)
    for c in range(ctx):
        scale = jnp.broadcast_to(factors[c] / denominator, (LANES, rows)).T
        merged += lat_all[c].astype(F32) * scale
    merged = merged.astype(BF16)
    for h in range(heads):
        part = lax.dot_general(
            merged[h * span : (h + 1) * span, :],
            kv_ref[h, NOPE:, :],
            nt,
            preferred_element_type=F32,
        )
        att_send[:, h * VDIM : (h + 1) * VDIM] = part.astype(BF16)
    copies = ctx_start(4, lambda peer: att_send, att_all)
    att_all[me_c] = att_send[...]
    finish(copies)
    attention = sum(att_all[c].astype(F32) for c in range(ctx)).astype(BF16)
    proj_send[...] = jnp.dot(attention, o_ref[...], preferred_element_type=F32).astype(BF16)
    copies = [
        pltpu.make_async_remote_copy(
            src_ref=proj_send,
            dst_ref=proj_all.at[me_s],
            send_sem=sub_send.at[d],
            recv_sem=sub_recv.at[d],
            device_id={"sub": lax.rem(me_s + d, sub)},
            device_id_type=MESH,
        )
        for d in range(1, sub)
    ]
    for copy in copies:
        copy.start()
    proj_all[me_s] = proj_send[...]
    residual = pack_all[:, :, heads * 2 * LANES : heads * 2 * LANES + quarter].reshape(span, quarter)
    finish(copies)
    hid_send[...] = residual + sum(proj_all[s].astype(F32) for s in range(sub))
    copies = ctx_start(5, lambda peer: hid_send, hid_all)
    hid_all[me_c] = hid_send[...]
    finish(copies)

    squares = sum(
        jnp.sum(hid_all[c] * hid_all[c], axis=1, keepdims=True) for c in range(ctx)
    )
    inverse_rms = lax.rsqrt(squares / (ctx * quarter) + epsilon)
    for c in range(ctx):
        cols = slice(c * quarter, (c + 1) * quarter)
        normed[:, cols] = (hid_all[c] * inverse_rms * gain_ref[:, cols]).astype(BF16)

    total[...] = jnp.zeros_like(total)
    comb = pack_all[:, :, heads * 2 * LANES + quarter :].reshape(span, LANES)
    comb_lane = lax.broadcasted_iota(jnp.int32, (span, LANES), 1)

    def expert(e, carry):
        slot = lax.rem(e, slots)
        gate_copy, up_copy, down_copy = weight_copies(e, slot)
        gate_copy.wait()
        gate_act = jnp.dot(normed[...], gate_buf[slot], preferred_element_type=F32)
        up_copy.wait()
        up_act = jnp.dot(normed[...], up_buf[slot], preferred_element_type=F32)
        gated = (gate_act / (1.0 + jnp.exp(-gate_act)) * up_act).astype(BF16)
        down_copy.wait()
        mix = jnp.sum(jnp.where(comb_lane == e, comb, 0.0), axis=1, keepdims=True)
        total[...] += mix * jnp.dot(gated, down_buf[slot], preferred_element_type=F32)
        return carry

    def expert_and_refill(e, carry):
        expert(e, carry)
        for copy in weight_copies(e + slots, lax.rem(e, slots)):
            copy.start()
        return carry

    lax.fori_loop(0, experts - slots, expert_and_refill, 0)
    lax.fori_loop(experts - slots, experts, expert, 0)

    for c in range(ctx):
        for s in range(sub):
            fin_send[c * sub + s] = total[
                c * tok : (c + 1) * tok, s * quarter : (s + 1) * quarter
            ].astype(BF16)
    copies = []
    for dc in range(ctx):
        for ds in range(sub):
            if dc or ds:
                peer_c, peer_s = lax.rem(me_c + dc, ctx), lax.rem(me_s + ds, sub)
                copies.append(
                    pltpu.make_async_remote_copy(
                        src_ref=fin_send.at[peer_c * sub + peer_s],
                        dst_ref=fin_all.at[me_c * sub + me_s],
                        send_sem=fin_ssem.at[dc * sub + ds],
                        recv_sem=fin_rsem.at[dc * sub + ds],
                        device_id={"ctx": peer_c, "sub": peer_s},
                        device_id_type=MESH,
                    )
                )
                copies[-1].start()
    me = me_c * sub + me_s
    fin_all[me] = fin_send[me]
    hidden = hid_all[me_s, pl.ds(pl.multiple_of(me_c * tok, tok), tok), :]
    finish(copies)
    routed = sum(fin_all[i].astype(F32) for i in range(ctx * sub))
    out_ref[...] = (hidden + routed).astype(out_ref.dtype)


def fused_body(
    queries,
    latent_cache,
    cache_len,
    kv_up,
    o_weight,
    residual,
    norm_gain,
    route_ids,
    route_weights,
    w_gate,
    w_up,
    w_down,
):
    ctx, sub = lax.axis_size("ctx"), lax.axis_size("sub")
    heads, tok, experts = kv_up.shape[0], queries.shape[0], w_gate.shape[0]
    span, rows, quarter = ctx * tok, heads * ctx * tok, o_weight.shape[1]
    width = residual.shape[1]
    slots = min(SLOTS, experts)
    q = queries.astype(F32).reshape(tok, heads, NOPE + ROPE)
    q = jnp.pad(q, ((0, 0), (0, 0), (0, 2 * LANES - NOPE - ROPE))).reshape(1, tok, heads * 2 * LANES)
    res = residual.astype(F32).reshape(tok, ctx, quarter).transpose(1, 0, 2)
    names = (
        lax.broadcasted_iota(jnp.int32, (ctx, 1, 1, LANES), 0) * experts
        + lax.broadcasted_iota(jnp.int32, (ctx, 1, 1, LANES), 3)
    )
    inside = lax.broadcasted_iota(jnp.int32, (ctx, 1, 1, LANES), 3) < experts
    hit = (route_ids[None, :, :, None] == names) & inside
    comb = jnp.sum(jnp.where(hit, route_weights[None, :, :, None], 0.0), axis=2)
    pack = jnp.concatenate([jnp.broadcast_to(q, (ctx,) + q.shape[1:]), res, comb], axis=2)
    count = latent_cache.shape[0]
    live = (lax.broadcasted_iota(jnp.int32, (1, count), 1) < cache_len[0]).astype(F32)
    gain = norm_gain.astype(F32).reshape(1, width)
    vmem = pl.BlockSpec(memory_space=pltpu.VMEM)
    hbm = pl.BlockSpec(memory_space=pl.ANY)
    dma = pltpu.SemaphoreType.DMA
    return pl.pallas_call(
        functools.partial(fused_kernel, (ctx, sub, tok, heads, experts, slots)),
        out_shape=jax.ShapeDtypeStruct((tok, width // sub), BF16),
        in_specs=[vmem] * 6 + [hbm] * 3,
        out_specs=vmem,
        scratch_shapes=[
            pltpu.VMEM(pack.shape, F32),
            pltpu.VMEM((rows, LANES), BF16),
            pltpu.VMEM((ctx, rows, LANES), BF16),
            pltpu.VMEM((ctx, rows, LANES), BF16),
            pltpu.VMEM((ctx, rows, LANES), BF16),
            pltpu.VMEM((16, rows), F32),
            pltpu.VMEM((ctx, 16, rows), F32),
            pltpu.VMEM((span, heads * VDIM), BF16),
            pltpu.VMEM((ctx, span, heads * VDIM), BF16),
            pltpu.VMEM((span, quarter), BF16),
            pltpu.VMEM((sub, span, quarter), BF16),
            pltpu.VMEM((span, quarter), F32),
            pltpu.VMEM((ctx, span, quarter), F32),
            pltpu.VMEM((span, width), BF16),
            pltpu.VMEM((span, width), F32),
            pltpu.VMEM((ctx * sub, tok, quarter), BF16),
            pltpu.VMEM((ctx * sub, tok, quarter), BF16),
            pltpu.VMEM((slots,) + w_gate.shape[1:], BF16),
            pltpu.VMEM((slots,) + w_up.shape[1:], BF16),
            pltpu.VMEM((slots,) + w_down.shape[1:], BF16),
            dma((6, ctx)),
            dma((6, ctx)),
            dma((sub,)),
            dma((sub,)),
            dma((ctx * sub,)),
            dma((ctx * sub,)),
            dma((slots, 3)),
        ],
        compiler_params=pltpu.CompilerParams(
            collective_id=0, has_side_effects=True, vmem_limit_bytes=67043328
        ),
    )(pack, live, latent_cache, kv_up, o_weight, gain, w_gate, w_up, w_down)


def choose_body(*args):
    kv_up, o_weight, w_gate = args[3], args[4], args[9]
    ctx, sub, tok = lax.axis_size("ctx"), lax.axis_size("sub"), args[0].shape[0]
    fits = (
        ctx == sub
        and kv_up.shape[2] == LANES
        and o_weight.shape[1] % LANES == 0
        and kv_up.shape[0] * ctx * tok == LANES
        and w_gate.shape[0] <= LANES
        and tok % 8 == 0
    )
    return fused_body(*args) if fits else body(*args)


def solution(mesh):
    in_specs = (
        P(("grp", "ctx"), "sub"),
        P(("grp", "ctx"), None),
        P(("grp", "ctx")),
        P(("grp", "sub"), None, "ctx"),
        P("sub", "ctx"),
        P(("grp", "ctx"), None),
        P(),
        P(("grp", "ctx"), None),
        P(("grp", "ctx"), None),
        P("ctx", None, "sub"),
        P("ctx", None, "sub"),
        P("ctx", "sub", None),
    )
    out_specs = P(("grp", "ctx"), "sub")
    return jax.shard_map(choose_body, mesh=mesh, in_specs=in_specs, out_specs=out_specs, check_vma=False)
```

```python
import functools

import jax
import jax.numpy as jnp
from jax import lax
from jax.experimental import pallas as pl
from jax.experimental.pallas import tpu as pltpu
from jax.sharding import PartitionSpec as P

D = 2048
NOPE = 128
ROPE = 64
VDIM = 128
LATENT = 512
TOP = 6
CAP = 2


epsilon = 1e-06


def local_attention(absorbed, cache_rows, length, up_value):
    scores = jnp.einsum("qhc,kc->qhk", absorbed, cache_rows, preferred_element_type=jnp.float32) * (
        NOPE + ROPE
    ) ** (-0.5)
    live_mask = lax.broadcasted_iota(jnp.int32, (cache_rows.shape[0],), 0) < length
    scores = jnp.where(live_mask[None, None, :], scores, -jnp.inf)
    highest = jnp.max(scores, axis=2)
    weights = jnp.exp(scores - highest[:, :, None]).astype(jnp.bfloat16)
    totals = jnp.sum(weights, axis=2, dtype=jnp.float32)
    latent_out = jnp.einsum(
        "qhk,kl->qhl", weights, cache_rows[:, :LATENT], preferred_element_type=jnp.float32
    ).astype(jnp.bfloat16)
    head_out = jnp.einsum("qhl,hvl->qhv", latent_out, up_value, preferred_element_type=jnp.float32)
    return (highest, totals, head_out)


def body(
    queries,
    latent_cache,
    cache_len,
    kv_up,
    o_weight,
    residual,
    norm_gain,
    route_ids,
    route_weights,
    w_gate,
    w_up,
    w_down,
):
    ctx_count = lax.axis_size("ctx")
    sub_count = lax.axis_size("sub")
    heads_dev = kv_up.shape[0]
    token_count = queries.shape[0]
    up_full = lax.all_gather(kv_up, "ctx", axis=2, tiled=True)
    up_key = up_full[:, :NOPE, :]
    up_value = up_full[:, NOPE:, :]
    own_rows = queries.reshape(token_count, heads_dev, NOPE + ROPE)
    query_latent = jnp.einsum(
        "qhn,hnl->qhl", own_rows[:, :, :NOPE], up_key, preferred_element_type=jnp.float32
    ).astype(jnp.bfloat16)
    mine = jnp.concatenate([query_latent, own_rows[:, :, NOPE:]], axis=2).reshape(
        token_count, heads_dev * (LATENT + ROPE)
    )
    absorbed = lax.all_gather(mine, "ctx", axis=0, tiled=True).reshape(-1, heads_dev, LATENT + ROPE)
    highest, totals, head_out = local_attention(absorbed, latent_cache, cache_len[0], up_value)
    all_rows = absorbed.shape[0]
    got_out, got_high, got_total = (
        lax.all_to_all(
            head_out.reshape(all_rows, heads_dev * VDIM),
            "ctx",
            split_axis=0,
            concat_axis=0,
            tiled=True,
        ),
        lax.all_to_all(highest, "ctx", split_axis=0, concat_axis=0, tiled=True),
        lax.all_to_all(totals, "ctx", split_axis=0, concat_axis=0, tiled=True),
    )
    got_out = got_out.reshape(ctx_count, token_count, heads_dev, VDIM)
    got_high = got_high.reshape(ctx_count, token_count, heads_dev)
    got_total = got_total.reshape(ctx_count, token_count, heads_dev)
    overall = jnp.max(got_high, axis=0)
    factor = jnp.exp(got_high - overall[None])
    numerator = jnp.sum(got_out * factor[:, :, :, None], axis=0)
    denominator = jnp.sum(got_total * factor, axis=0)
    attention = (
        (numerator / denominator[:, :, None])
        .astype(jnp.bfloat16)
        .reshape(token_count, heads_dev * VDIM)
    )
    projected = jnp.dot(
        attention,
        lax.all_gather(o_weight, "ctx", axis=1, tiled=True),
        preferred_element_type=jnp.float32,
    )
    quarter = D // sub_count
    offset_cols = lax.axis_index("sub") * quarter
    hidden = residual.astype(jnp.float32) + lax.psum(projected.astype(jnp.bfloat16), "sub").astype(
        jnp.float32
    )
    inverse_rms = lax.rsqrt(jnp.mean(hidden * hidden, axis=1) + epsilon)
    normed = (hidden * inverse_rms[:, None] * norm_gain.astype(jnp.float32)).astype(jnp.bfloat16)
    hidden_part = lax.dynamic_slice_in_dim(hidden, offset_cols, quarter, 1)
    experts_dev = w_gate.shape[0]
    expert_total = experts_dev * ctx_count
    pair_count = token_count * TOP
    expert_ids = route_ids.reshape(pair_count)
    onehot = (expert_ids[:, None] == lax.broadcasted_iota(jnp.int32, (1, expert_total), 1)).astype(
        jnp.int32
    )
    earlier = jnp.cumsum(onehot, axis=0) - onehot
    slot_ids = jnp.sum(earlier * onehot, axis=1)
    targets = (expert_ids * CAP + slot_ids).reshape(token_count, TOP)
    matches = targets[:, :, None] == lax.broadcasted_iota(jnp.int32, (1, 1, expert_total * CAP), 2)
    select = jnp.sum(matches.astype(jnp.int32), axis=1).astype(jnp.bfloat16)
    outgoing = jnp.einsum("tj,td->jd", select, normed, preferred_element_type=jnp.float32).astype(
        jnp.bfloat16
    )
    outgoing = outgoing.reshape(ctx_count, experts_dev, CAP, D)
    received = lax.all_to_all(outgoing, "ctx", split_axis=0, concat_axis=0, tiled=True)
    gate_act = jnp.einsum("sekd,edf->sekf", received, w_gate, preferred_element_type=jnp.float32)
    up_act = jnp.einsum("sekd,edf->sekf", received, w_up, preferred_element_type=jnp.float32)
    gated_rows = (jax.nn.silu(gate_act) * up_act).astype(jnp.bfloat16)
    partial_out = jnp.einsum(
        "sekf,efd->sekd", gated_rows, w_down, preferred_element_type=jnp.float32
    )
    summed = lax.psum_scatter(
        partial_out.astype(jnp.bfloat16), "sub", scatter_dimension=3, tiled=True
    )
    back_rows = lax.all_to_all(summed, "ctx", split_axis=0, concat_axis=0, tiled=True)
    back_rows = back_rows.reshape(expert_total * CAP, quarter)
    mixing = jnp.sum(jnp.where(matches, route_weights[:, :, None], 0.0), axis=1)
    routed = jnp.dot(mixing, back_rows.astype(jnp.float32), precision=lax.Precision.HIGHEST)
    return (hidden_part + routed).astype(jnp.bfloat16)


LANES = 128
SLOTS = 12
MESH = pl.DeviceIdType.MESH
F32 = jnp.float32
BF16 = jnp.bfloat16


def fused_kernel(
    dims,
    q_ref,
    res_ref,
    ids_ref,
    mix_ref,
    live_ref,
    cache_ref,
    kv_ref,
    o_ref,
    gain_ref,
    gate_hbm,
    up_hbm,
    down_hbm,
    out_ref,
    q_all,
    res_all,
    comb_send,
    comb_all,
    ql_send,
    ql_all,
    lat_send,
    lat_all,
    stat_send,
    stat_all,
    att_send,
    att_all,
    proj_send,
    proj_all,
    hid_send,
    hid_all,
    normed,
    total,
    fin_send,
    fin_all,
    gate_buf,
    up_buf,
    down_buf,
    ctx_send,
    ctx_recv,
    sub_send,
    sub_recv,
    fin_ssem,
    fin_rsem,
    w_sem,
):
    ctx, sub, tok, heads, experts, slots = dims
    me_c = lax.axis_index("ctx")
    me_s = lax.axis_index("sub")
    span = ctx * tok
    rows = heads * span
    quarter = o_ref.shape[1]

    def weight_copies(e, slot):
        return (
            pltpu.make_async_copy(gate_hbm.at[e], gate_buf.at[slot], w_sem.at[slot, 0]),
            pltpu.make_async_copy(up_hbm.at[e], up_buf.at[slot], w_sem.at[slot, 1]),
            pltpu.make_async_copy(down_hbm.at[e], down_buf.at[slot], w_sem.at[slot, 2]),
        )

    def prefetch(e, carry):
        for copy in weight_copies(e, e):
            copy.start()
        return carry

    lax.fori_loop(0, slots, prefetch, 0)

    barrier = pltpu.get_barrier_semaphore()
    for dc in range(ctx):
        for ds in range(sub):
            if dc or ds:
                pl.semaphore_signal(
                    barrier,
                    inc=1,
                    device_id={"ctx": lax.rem(me_c + dc, ctx), "sub": lax.rem(me_s + ds, sub)},
                    device_id_type=MESH,
                )
    pl.semaphore_wait(barrier, ctx * sub - 1)

    def ctx_copy(phase, source_of, target, d):
        peer = lax.rem(me_c + d, ctx)
        return pltpu.make_async_remote_copy(
            src_ref=source_of(peer),
            dst_ref=target.at[me_c],
            send_sem=ctx_send.at[phase, d],
            recv_sem=ctx_recv.at[phase, d],
            device_id={"ctx": peer},
            device_id_type=MESH,
        )

    def ctx_start(phase, source_of, target):
        copies = [ctx_copy(phase, source_of, target, d) for d in range(1, ctx)]
        for copy in copies:
            copy.start()
        return copies

    def finish(copies):
        for copy in copies:
            copy.wait()

    def own_columns(peer):
        return pl.ds(pl.multiple_of(peer * quarter, quarter), quarter)

    copies = ctx_start(0, lambda peer: q_ref, q_all)
    early = ctx_start(6, lambda peer: res_ref.at[:, own_columns(peer)], res_all)
    q_all[me_c] = q_ref[...]
    res_all[me_c] = res_ref[:, own_columns(me_c)]
    lane = lax.broadcasted_iota(jnp.int32, (tok, LANES), 1)
    ids, mixes = ids_ref[...], mix_ref[...]
    for c in range(ctx):
        comb = jnp.zeros((tok, LANES), F32)
        for k in range(TOP):
            hit = (ids[:, k : k + 1] == lane + c * experts) & (lane < experts)
            comb += jnp.where(hit, mixes[:, k : k + 1], 0.0)
        comb_send[c] = comb
    early += ctx_start(7, lambda peer: comb_send.at[peer], comb_all)
    comb_all[me_c] = comb_send[me_c]
    finish(copies)

    per_head = NOPE + ROPE
    q_rows = q_all[...].astype(F32).reshape(span, heads * per_head)
    turned = [
        q_rows if h == 0 else pltpu.roll(q_rows, (heads - h) * per_head, 1) for h in range(heads)
    ]
    for h in range(heads):
        nope = turned[h][:, :NOPE].astype(BF16)
        part = jnp.dot(nope, kv_ref[h, :NOPE, :], preferred_element_type=F32).astype(BF16)
        ql_send[h * span : (h + 1) * span, :] = part
    copies = ctx_start(1, lambda peer: ql_send, ql_all)
    ql_all[me_c] = ql_send[...]
    rope = jnp.concatenate(
        [turned[h][:, NOPE:per_head] for h in range(heads)],
        axis=0,
    ).astype(BF16)
    nt = (((1,), (1,)), ((), ()))
    rope_scores = jnp.dot(rope, cache_ref[LATENT:, :], preferred_element_type=F32)
    finish(copies)
    lat_q = jnp.concatenate([ql_all[c] for c in range(ctx)], axis=1)
    scores = jnp.dot(lat_q, cache_ref[:LATENT, :], preferred_element_type=F32)
    scores = (scores + rope_scores) * (NOPE + ROPE) ** (-0.5)
    scores = jnp.where(live_ref[...] > 0.0, scores, -jnp.inf)
    highest = jnp.max(scores, axis=1, keepdims=True)
    weights = jnp.exp(scores - highest).astype(BF16)
    totals = jnp.sum(weights.astype(F32), axis=1, keepdims=True)
    lane = lax.broadcasted_iota(jnp.int32, (rows, LANES), 1)
    stats = jnp.where(lane < 64, highest, totals).T
    stat_send[0:8, :] = stats[0:8, :]
    stat_send[8:16, :] = stats[64:72, :]
    copies = ctx_start(3, lambda peer: stat_send, stat_all)
    stat_all[me_c] = stat_send[...]
    latent = lax.dot_general(
        weights, cache_ref[:LATENT, :], nt, preferred_element_type=F32
    ).astype(BF16)
    for c in range(ctx):
        lat_send[c] = latent[:, c * LANES : (c + 1) * LANES]
    copies += ctx_start(2, lambda peer: lat_send.at[peer], lat_all)
    lat_all[me_c] = lat_send[me_c]
    finish(copies)

    highs = [stat_all[c, 0:1, :] for c in range(ctx)]
    overall = functools.reduce(jnp.maximum, highs)
    factors = [jnp.exp(high - overall) for high in highs]
    denominator = sum(f * stat_all[c, 8:9, :] for c, f in enumerate(factors))
    merged = jnp.zeros((rows, LANES), F32)
    for c in range(ctx):
        scale = jnp.broadcast_to(factors[c] / denominator, (LANES, rows)).T
        merged += lat_all[c].astype(F32) * scale
    merged = merged.astype(BF16)
    for h in range(heads):
        part = lax.dot_general(
            merged[h * span : (h + 1) * span, :],
            kv_ref[h, NOPE:, :],
            nt,
            preferred_element_type=F32,
        )
        att_send[:, h * VDIM : (h + 1) * VDIM] = part.astype(BF16)
    copies = ctx_start(4, lambda peer: att_send, att_all)
    att_all[me_c] = att_send[...]
    finish(copies)
    attention = sum(att_all[c].astype(F32) for c in range(ctx)).astype(BF16)
    proj_send[...] = jnp.dot(attention, o_ref[...], preferred_element_type=F32).astype(BF16)
    copies = [
        pltpu.make_async_remote_copy(
            src_ref=proj_send,
            dst_ref=proj_all.at[me_s],
            send_sem=sub_send.at[d],
            recv_sem=sub_recv.at[d],
            device_id={"sub": lax.rem(me_s + d, sub)},
            device_id_type=MESH,
        )
        for d in range(1, sub)
    ]
    for copy in copies:
        copy.start()
    proj_all[me_s] = proj_send[...]
    finish(copies + early)
    residual = res_all[...].astype(F32).reshape(span, quarter)
    hid_send[...] = residual + sum(proj_all[s].astype(F32) for s in range(sub))
    copies = ctx_start(5, lambda peer: hid_send, hid_all)
    hid_all[me_c] = hid_send[...]
    finish(copies)

    squares = sum(
        jnp.sum(hid_all[c] * hid_all[c], axis=1, keepdims=True) for c in range(ctx)
    )
    inverse_rms = lax.rsqrt(squares / (ctx * quarter) + epsilon)
    for c in range(ctx):
        cols = slice(c * quarter, (c + 1) * quarter)
        normed[:, cols] = (hid_all[c] * inverse_rms * gain_ref[:, cols]).astype(BF16)

    total[...] = jnp.zeros_like(total)
    comb = comb_all[...].reshape(span, LANES)
    comb_lane = lax.broadcasted_iota(jnp.int32, (span, LANES), 1)

    def expert(e, carry):
        slot = lax.rem(e, slots)
        gate_copy, up_copy, down_copy = weight_copies(e, slot)
        gate_copy.wait()
        gate_act = lax.dot_general(normed[...], gate_buf[slot], nt, preferred_element_type=F32)
        up_copy.wait()
        up_act = lax.dot_general(normed[...], up_buf[slot], nt, preferred_element_type=F32)
        gated = (gate_act / (1.0 + jnp.exp(-gate_act)) * up_act).astype(BF16)
        down_copy.wait()
        mix = jnp.sum(jnp.where(comb_lane == e, comb, 0.0), axis=1, keepdims=True)
        total[...] += mix * jnp.dot(gated, down_buf[slot], preferred_element_type=F32)
        return carry

    def expert_and_refill(e, carry):
        expert(e, carry)
        for copy in weight_copies(e + slots, lax.rem(e, slots)):
            copy.start()
        return carry

    lax.fori_loop(0, experts - slots, expert_and_refill, 0)
    lax.fori_loop(experts - slots, experts, expert, 0)

    for c in range(ctx):
        for s in range(sub):
            fin_send[c * sub + s] = total[
                c * tok : (c + 1) * tok, s * quarter : (s + 1) * quarter
            ].astype(BF16)
    copies = []
    for dc in range(ctx):
        for ds in range(sub):
            if dc or ds:
                peer_c, peer_s = lax.rem(me_c + dc, ctx), lax.rem(me_s + ds, sub)
                copies.append(
                    pltpu.make_async_remote_copy(
                        src_ref=fin_send.at[peer_c * sub + peer_s],
                        dst_ref=fin_all.at[me_c * sub + me_s],
                        send_sem=fin_ssem.at[dc * sub + ds],
                        recv_sem=fin_rsem.at[dc * sub + ds],
                        device_id={"ctx": peer_c, "sub": peer_s},
                        device_id_type=MESH,
                    )
                )
                copies[-1].start()
    me = me_c * sub + me_s
    fin_all[me] = fin_send[me]
    hidden = hid_all[me_s, pl.ds(pl.multiple_of(me_c * tok, tok), tok), :]
    finish(copies)
    routed = sum(fin_all[i].astype(F32) for i in range(ctx * sub))
    out_ref[...] = (hidden + routed).astype(out_ref.dtype)


def fused_body(
    queries,
    latent_cache,
    cache_len,
    kv_up,
    o_weight,
    residual,
    norm_gain,
    route_ids,
    route_weights,
    w_gate,
    w_up,
    w_down,
):
    ctx, sub = lax.axis_size("ctx"), lax.axis_size("sub")
    heads, tok, experts = kv_up.shape[0], queries.shape[0], w_gate.shape[0]
    span, rows, quarter = ctx * tok, heads * ctx * tok, o_weight.shape[1]
    width = residual.shape[1]
    slots = min(SLOTS, experts)
    w_gate, w_up = jnp.swapaxes(w_gate, 1, 2), jnp.swapaxes(w_up, 1, 2)
    count = latent_cache.shape[0]
    live = (lax.broadcasted_iota(jnp.int32, (1, count), 1) < cache_len[0]).astype(F32)
    gain = norm_gain.astype(F32).reshape(1, width)
    vmem = pl.BlockSpec(memory_space=pltpu.VMEM)
    hbm = pl.BlockSpec(memory_space=pl.ANY)
    dma = pltpu.SemaphoreType.DMA
    return pl.pallas_call(
        functools.partial(fused_kernel, (ctx, sub, tok, heads, experts, slots)),
        out_shape=jax.ShapeDtypeStruct((tok, width // sub), BF16),
        in_specs=[vmem] * 9 + [hbm] * 3,
        out_specs=vmem,
        scratch_shapes=[
            pltpu.VMEM((ctx,) + queries.shape, BF16),
            pltpu.VMEM((ctx, tok, quarter), BF16),
            pltpu.VMEM((ctx, tok, LANES), F32),
            pltpu.VMEM((ctx, tok, LANES), F32),
            pltpu.VMEM((rows, LANES), BF16),
            pltpu.VMEM((ctx, rows, LANES), BF16),
            pltpu.VMEM((ctx, rows, LANES), BF16),
            pltpu.VMEM((ctx, rows, LANES), BF16),
            pltpu.VMEM((16, rows), F32),
            pltpu.VMEM((ctx, 16, rows), F32),
            pltpu.VMEM((span, heads * VDIM), BF16),
            pltpu.VMEM((ctx, span, heads * VDIM), BF16),
            pltpu.VMEM((span, quarter), BF16),
            pltpu.VMEM((sub, span, quarter), BF16),
            pltpu.VMEM((span, quarter), F32),
            pltpu.VMEM((ctx, span, quarter), F32),
            pltpu.VMEM((span, width), BF16),
            pltpu.VMEM((span, width), F32),
            pltpu.VMEM((ctx * sub, tok, quarter), BF16),
            pltpu.VMEM((ctx * sub, tok, quarter), BF16),
            pltpu.VMEM((slots,) + w_gate.shape[1:], BF16),
            pltpu.VMEM((slots,) + w_up.shape[1:], BF16),
            pltpu.VMEM((slots,) + w_down.shape[1:], BF16),
            dma((8, ctx)),
            dma((8, ctx)),
            dma((sub,)),
            dma((sub,)),
            dma((ctx * sub,)),
            dma((ctx * sub,)),
            dma((slots, 3)),
        ],
        compiler_params=pltpu.CompilerParams(
            collective_id=0, has_side_effects=True, vmem_limit_bytes=67043328
        ),
    )(
        queries,
        residual,
        route_ids,
        route_weights,
        live,
        latent_cache.T,
        kv_up,
        o_weight,
        gain,
        w_gate,
        w_up,
        w_down,
    )


def choose_body(*args):
    kv_up, o_weight, w_gate = args[3], args[4], args[9]
    ctx, sub, tok = lax.axis_size("ctx"), lax.axis_size("sub"), args[0].shape[0]
    fits = (
        ctx == sub
        and kv_up.shape[2] == LANES
        and o_weight.shape[1] % LANES == 0
        and kv_up.shape[0] * ctx * tok == LANES
        and w_gate.shape[0] <= LANES
        and tok % 8 == 0
    )
    return fused_body(*args) if fits else body(*args)


def solution(mesh):
    in_specs = (
        P(("grp", "ctx"), "sub"),
        P(("grp", "ctx"), None),
        P(("grp", "ctx")),
        P(("grp", "sub"), None, "ctx"),
        P("sub", "ctx"),
        P(("grp", "ctx"), None),
        P(),
        P(("grp", "ctx"), None),
        P(("grp", "ctx"), None),
        P("ctx", None, "sub"),
        P("ctx", None, "sub"),
        P("ctx", "sub", None),
    )
    out_specs = P(("grp", "ctx"), "sub")
    return jax.shard_map(choose_body, mesh=mesh, in_specs=in_specs, out_specs=out_specs, check_vma=False)
```
